32 devices in a mesh: group: 8 (over z, y), proc: 4 (over x, core).
Axes of the slice: x: 2, y: 2, z: 4, core: 2. Of those that a mesh axis runs over, the one named last changes fastest.
Arguments:
- ancestor_rows: bfloat16 [32, 256, 8192], P('group', 'proc'), may hold values from -6 to 6
- piece_owner: int32 [32], replicated, may hold values from 0 to 31, each once
- structure: int32 [8, 8], replicated, may hold values from 0 to 15, as said below
- kept_blocks: int32 [8, 7], replicated, may hold values from 0 to 7, as said below
- panel_parent: bfloat16 [8, 8, 2, 256, 512], P('group', None, None, 'proc'), may hold values from -0.09375 to 0.09375
- panel_child: bfloat16 [8, 8, 2, 256, 512], P('group', None, None, 'proc'), may hold values from -0.09375 to 0.09375
- pivot_parent: bfloat16 [8, 2, 256, 512], P('group', None, 'proc'), may hold values from -4 to 6, as said below
- pivot_child: bfloat16 [8, 2, 256, 512], P('group', None, 'proc'), may hold values from -4 to 6, as said below
Outputs:
- column_parent: bfloat16 [8, 8, 2, 256, 512], P('group', None, None, 'proc')
- block_parent: bfloat16 [8, 2, 256, 512], P('group', None, 'proc')
- column_child: bfloat16 [8, 8, 2, 256, 512], P('group', None, None, 'proc')
- block_child: bfloat16 [8, 2, 256, 512], P('group', None, 'proc')
The draws below stay inside these ranges and needn't reach their ends.
Inputs may be any that keep to these rules, and one draw needn't show every extreme that they name: `structure`: each row names 8 different top supernodes in increasing order. `kept_blocks`: each row names 7 different positions in increasing order. `piece_owner`: a permutation. `pivot_parent`: each group's block, read as a 512 x 512 matrix, is symmetric. `pivot_child`: each group's block, read as a 512 x 512 matrix, is symmetric.
All inputs are finite; a program needn't handle non-finite values.
Results may differ from the reference program's by a relative error of at most 0.018.
Values may be sent and summed in bfloat16 or wider, within the bound.
A program may use at most 128 MiB of HBM per device.

```python
import jax
import jax.numpy as jnp
from jax import lax

W = 512
RB = 8
NT = 16
PIECES = 2
GROUPS = 8


def draw_structure(key, part):
    heat_key, noise_key = jax.random.split(jax.random.fold_in(key, 101))
    heat = jax.random.randint(heat_key, (NT,), 0, 4)
    noise = jax.random.randint(noise_key, (GROUPS, NT), 0, 6)
    score = (noise + 3 * heat[None, :]) * NT + jnp.arange(NT)[None, :]
    chosen = lax.top_k(score, RB)[1]
    return jnp.sort(chosen, axis=1).astype(jnp.int32)


def draw_kept_blocks(key, part):
    dropped = jax.random.randint(jax.random.fold_in(key, 202), (GROUPS, 1), 0, RB)
    positions = jnp.arange(RB - 1)[None, :]
    return (positions + (positions >= dropped).astype(jnp.int32)).astype(jnp.int32)


def symmetric_pivot(key):
    sample = jnp.clip(jax.random.normal(key, (GROUPS, W, W), jnp.float32), -4.0, 4.0)
    symmetric = 0.5 * (sample + jnp.swapaxes(sample, 1, 2)) + 2.0 * jnp.eye(W, dtype=jnp.float32)[None]
    return symmetric.reshape(GROUPS, PIECES, W // PIECES, W).astype(jnp.bfloat16)


def draw_pivot_parent(key, part):
    return symmetric_pivot(jax.random.fold_in(key, 303))


def draw_pivot_child(key, part):
    return symmetric_pivot(jax.random.fold_in(key, 404))


def block_levels(stream_key, dims, pieces, least, largest):
    gain, own = 1.0, jax.random.fold_in(stream_key, 6)
    for dim, blocks in pieces:
        draws = jnp.exp(jax.random.uniform(jax.random.fold_in(own, dim), (blocks,), jnp.float32, least / len(pieces), largest / len(pieces)))
        gain = gain * jnp.repeat(draws, dims[dim] // blocks).reshape([-1 if axis == dim else 1 for axis in range(len(dims))])
    return gain


def normal_values(key, shape, scale, limit, pieces=(), kind=jnp.bfloat16):
    loudness = block_levels(key, shape, pieces, -0.22, 0.18) if pieces else 1.0
    drawn = jax.random.normal(key, shape, jnp.float32) * scale * loudness
    return jnp.minimum(jnp.maximum(drawn, -limit), limit).astype(kind)


def setup_inputs(seed: int = 0) -> dict:
    arg_keys = jax.random.split(jax.random.key(seed), 9)
    return {
        "ancestor_rows": normal_values(arg_keys[0], (NT * PIECES, W // PIECES, NT * W), 1.0, 6.0, ((0, 8), (1, 4))),
        "piece_owner": jax.random.permutation(arg_keys[1], NT * PIECES).astype(jnp.int32),
        "structure": draw_structure(jax.random.fold_in(arg_keys[8], 71), 0),
        "kept_blocks": draw_kept_blocks(jax.random.fold_in(arg_keys[8], 71), 0),
        "panel_parent": normal_values(arg_keys[4], (GROUPS, RB, PIECES, W // PIECES, W), (RB * W) ** -0.5, 0.09375, ((0, 8), (3, 4))),
        "panel_child": normal_values(arg_keys[5], (GROUPS, RB, PIECES, W // PIECES, W), (RB * W) ** -0.5, 0.09375, ((0, 8), (3, 4))),
        "pivot_parent": draw_pivot_parent(jax.random.fold_in(arg_keys[8], 71), 0),
        "pivot_child": draw_pivot_child(jax.random.fold_in(arg_keys[8], 71), 0),
    }


def product(left_side, right_side):
    return jnp.dot(left_side, right_side, preferred_element_type=jnp.float32, precision=lax.Precision.HIGHEST)


def reference(ancestor_rows, piece_owner, structure, kept_blocks, panel_parent, panel_child, pivot_parent, pivot_child):
    ancestor = ancestor_rows[piece_owner].reshape(NT, W, NT, W)
    order = RB * W

    def per_group(inputs):
        own_structure, kept_positions, first_panel, second_panel, first_pivot, second_pivot = inputs
        upper = ancestor[own_structure][:, :, own_structure, :].astype(jnp.float32).reshape(order, order)
        lower_first = first_panel.astype(jnp.float32).reshape(order, W)
        column_first = (-product(upper, lower_first)).astype(jnp.bfloat16)
        block_first = (first_pivot.astype(jnp.float32).reshape(W, W) - product(lower_first.T, column_first.astype(jnp.float32))).astype(jnp.bfloat16)
        stacked = jnp.concatenate([block_first[None], column_first.reshape(RB, W, W)[kept_positions]], axis=0).astype(jnp.float32)
        lower_second = second_panel.astype(jnp.float32).reshape(order, W)
        first_rows = product(stacked.reshape(order, W).T, lower_second)
        inner = upper.reshape(RB, W, RB, W)[kept_positions][:, :, kept_positions, :].reshape((RB - 1) * W, (RB - 1) * W)
        other_rows = product(stacked[1:].reshape((RB - 1) * W, W), lower_second[:W]) + product(inner, lower_second[W:])
        column_second = (-jnp.concatenate([first_rows, other_rows], axis=0)).astype(jnp.bfloat16)
        block_second = (second_pivot.astype(jnp.float32).reshape(W, W) - product(lower_second.T, column_second.astype(jnp.float32))).astype(jnp.bfloat16)
        return (column_first.reshape(RB, PIECES, W // PIECES, W), block_first.reshape(PIECES, W // PIECES, W),
                column_second.reshape(RB, PIECES, W // PIECES, W), block_second.reshape(PIECES, W // PIECES, W))

    results = lax.map(per_group, (structure, kept_blocks, panel_parent, panel_child, pivot_parent, pivot_child))
    return (results[0], results[1], results[2], results[3])
```

```python
import functools

import jax
import jax.numpy as jnp
from jax import lax
from jax.experimental import pallas as pl
from jax.experimental.pallas import tpu as pltpu
from jax.sharding import PartitionSpec as P


def product_kernel(strip_count, columns_ref, *refs):
    strips, panel_ref = refs[:strip_count], refs[strip_count]
    out_ref, total = refs[strip_count + 1 :]
    step = pl.program_id(0)

    @pl.when(step == 0)
    def _():
        total[...] = jnp.zeros_like(total)

    panel = panel_ref[...]
    for j, strip in enumerate(strips):
        total[j] += jnp.dot(strip[...], panel, preferred_element_type=jnp.float32)

    @pl.when(step == pl.num_programs(0) - 1)
    def _():
        out_ref[...] = total[...].astype(out_ref.dtype)


def structured_product(columns, strips, panel):
    blocks = columns.shape[0]
    rows = strips[0].shape[0]
    depth, width = panel.shape
    block = depth // blocks
    count = len(strips)
    return pl.pallas_call(
        functools.partial(product_kernel, count),
        out_shape=jax.ShapeDtypeStruct((count, rows, width), jnp.bfloat16),
        grid_spec=pltpu.PrefetchScalarGridSpec(
            num_scalar_prefetch=1,
            grid=(blocks,),
            in_specs=[pl.BlockSpec((rows, block), lambda b, c: (0, c[b]))] * count
            + [pl.BlockSpec((block, width), lambda b, c: (b, 0))],
            out_specs=pl.BlockSpec((count, rows, width), lambda b, c: (0, 0, 0)),
            scratch_shapes=[pltpu.VMEM((count, rows, width), jnp.float32)],
        ),
        compiler_params=pltpu.CompilerParams(dimension_semantics=("arbitrary",)),
        cost_estimate=pl.CostEstimate(
            flops=2 * count * rows * depth * width,
            bytes_accessed=2 * (count * rows * depth + depth * width + count * rows * width),
            transcendentals=0,
        ),
    )(columns, *strips, panel)


def per_device(
    groups,
    procs,
    ancestor_rows,
    piece_owner,
    structure,
    kept_blocks,
    panel_parent,
    panel_child,
    pivot_parent,
    pivot_child,
):
    f32, bf16 = jnp.float32, jnp.bfloat16
    group_index = lax.axis_index("group")
    proc_index = lax.axis_index("proc")
    owned_count, strip_rows, top_width = ancestor_rows.shape
    blocks = structure.shape[1]
    pieces = panel_parent.shape[2]
    width = panel_parent.shape[-1]
    slice_width = width // procs
    kept = kept_blocks.shape[1]
    own_structure = structure[group_index]
    kept_positions = kept_blocks[group_index]

    order = list(range(0, groups, 2)) + list(range(groups - 1, 0, -2))
    place_of = [order.index(g) for g in range(groups)]
    order_array = jnp.array(order, jnp.int32)
    place_array = jnp.array(place_of, jnp.int32)
    place = place_array[group_index]

    def shift(value, distance):
        pairs = [(order[i], order[(i + distance) % groups]) for i in range(groups)]
        return lax.ppermute(value, "group", pairs)

    def to_slices(panel):
        shape = panel.shape[:-1]
        view = panel.reshape(shape + (pieces, procs, strip_rows))
        return jnp.swapaxes(view, -3, -2).reshape(shape + (procs, slice_width))

    local_parent, local_child = panel_parent[0], panel_child[0]
    positions = jnp.arange(blocks, dtype=jnp.int32)
    match = kept_positions[None, :] == positions[:, None]
    source_block = jnp.sum(match * jnp.arange(1, kept + 1, dtype=jnp.int32)[None, :], axis=1)
    met = jnp.any(match, axis=1)
    placed_child = jnp.where(
        met[:, None, None, None], local_child[source_block], jnp.zeros((), bf16)
    )
    packed = jnp.concatenate([to_slices(local_parent), to_slices(placed_child)], axis=-1)
    panel = lax.all_to_all(packed, "proc", split_axis=3, concat_axis=2, tiled=True)
    panel = panel.reshape(blocks * width, 2 * slice_width)

    strips, offsets = [ancestor_rows.reshape(owned_count * strip_rows, top_width)], [0]
    bit = procs // 2
    while bit:
        pairs = [(q, q ^ bit) for q in range(procs)]
        strips = strips + [lax.ppermute(strip, "proc", pairs) for strip in strips]
        offsets = offsets + [offset ^ bit for offset in offsets]
        bit //= 2

    whole_parent = lax.all_gather(local_parent, "proc", axis=2, tiled=True).reshape(-1, width)
    whole_child = lax.all_gather(local_child, "proc", axis=2, tiled=True).reshape(-1, width)

    def send_home(arrived, distance):
        columns = structure[order_array[(place - distance) % groups]]
        return shift(structured_product(columns, strips, arrived), -distance)

    received = [None] * groups
    received[0] = structured_product(own_structure, strips, panel)
    forth = back = panel
    half = panel.shape[0] // 2
    for distance in range(1, groups // 2):
        forth, back = shift(forth, 1), shift(back, -1)
        received[distance] = send_home(forth, distance)
        received[groups - distance] = send_home(back, groups - distance)
    opposite = jnp.concatenate([shift(forth[:half], 1), shift(back[half:], -1)], axis=0)
    received[groups // 2] = send_home(opposite, groups // 2)

    gathered = jnp.stack(received).reshape(
        groups * procs * owned_count, strip_rows, 2 * slice_width
    )
    wanted = own_structure[:, None] * pieces + jnp.arange(pieces, dtype=jnp.int32)[None, :]
    slab_index = piece_owner[wanted]
    ahead = (place_array[slab_index // owned_count] - place) % groups
    within = slab_index % owned_count
    strip_slot = {offset: j for j, offset in enumerate(offsets)}
    slot_array = jnp.array([strip_slot[offset] for offset in range(procs)], jnp.int32)
    slots = slot_array[jnp.arange(procs, dtype=jnp.int32) ^ proc_index]
    index = (ahead[:, :, None] * procs + slots[None, None, :]) * owned_count + within[:, :, None]
    products = gathered[index.reshape(-1)].reshape(
        blocks, pieces, procs, strip_rows, 2 * slice_width
    )
    column_slice = -products[..., :slice_width]
    inner_slice = products[..., slice_width:]

    def to_strips(value):
        lead = value.shape[:-3]
        moved = lax.all_to_all(
            value, "proc", split_axis=len(lead), concat_axis=len(lead), tiled=True
        )
        moved = jnp.moveaxis(moved, -3, -2).reshape(
            lead + (strip_rows, procs, pieces, strip_rows)
        )
        return jnp.swapaxes(moved, -3, -2).reshape(lead + (strip_rows, width))

    both = to_strips(jnp.stack([column_slice, inner_slice]))
    column_parent, inner = both[0], both[1]

    flat_column = column_slice.reshape(blocks * width, slice_width)
    product_block = lax.dot_general(
        whole_parent, flat_column, (((0,), (0,)), ((), ())), preferred_element_type=f32
    )
    pivot_slice = pivot_parent[0].reshape(slice_width, width).T
    block_slice = (pivot_slice.astype(f32) - product_block).astype(bf16)
    block_parent = to_strips(block_slice.reshape(pieces, procs, strip_rows, slice_width))

    head_slice = jnp.concatenate(
        [
            block_slice[None],
            column_slice.reshape(blocks, width, slice_width)[kept_positions],
        ],
        axis=0,
    ).reshape(-1, slice_width)
    first_rows = lax.dot_general(
        head_slice, whole_child, (((0,), (0,)), ((), ())), preferred_element_type=f32
    ).reshape(1, pieces, strip_rows, width)

    head_rows = column_parent[kept_positions].reshape(-1, width)
    outer = jnp.dot(head_rows, whole_child[:width], preferred_element_type=f32)
    rest = outer.reshape(kept, pieces, strip_rows, width) + inner[kept_positions].astype(f32)
    column_child = (-jnp.concatenate([first_rows, rest], axis=0)).astype(bf16)

    partial = lax.dot_general(
        local_child.reshape(-1, width),
        column_child.reshape(-1, width),
        (((0,), (0,)), ((), ())),
        preferred_element_type=f32,
    ).astype(bf16)
    partial = lax.all_to_all(
        partial.reshape(pieces, procs, strip_rows, width),
        "proc",
        split_axis=1,
        concat_axis=1,
        tiled=True,
    )
    summed = jnp.sum(partial.astype(f32), axis=1)
    block_child = (pivot_child[0].astype(f32) - summed).astype(bf16)
    return column_parent[None], block_parent[None], column_child[None], block_child[None]


def solution(mesh):
    in_specs = (
        P("group", "proc", None),
        P(),
        P(),
        P(),
        P("group", None, None, "proc", None),
        P("group", None, None, "proc", None),
        P("group", None, "proc", None),
        P("group", None, "proc", None),
    )
    out_specs = (
        P("group", None, None, "proc", None),
        P("group", None, "proc", None),
        P("group", None, None, "proc", None),
        P("group", None, "proc", None),
    )
    body = functools.partial(per_device, mesh.shape["group"], mesh.shape["proc"])
    return jax.shard_map(
        body, mesh=mesh, in_specs=in_specs, out_specs=out_specs, check_vma=False
    )
```

```python
import functools

import jax
import jax.numpy as jnp
from jax import lax
from jax.experimental import pallas as pl
from jax.experimental.pallas import tpu as pltpu
from jax.sharding import PartitionSpec as P


def product_kernel(strip_count, columns_ref, *refs):
    strips, panel_ref = refs[:strip_count], refs[strip_count]
    out_ref, total = refs[strip_count + 1 :]
    step = pl.program_id(0)

    @pl.when(step == 0)
    def _():
        total[...] = jnp.zeros_like(total)

    panel = panel_ref[...]
    for j, strip in enumerate(strips):
        total[j] += jnp.dot(strip[...], panel, preferred_element_type=jnp.float32)

    @pl.when(step == pl.num_programs(0) - 1)
    def _():
        out_ref[...] = total[...].astype(out_ref.dtype)


def structured_product(columns, strips, panel):
    blocks = columns.shape[0]
    rows = strips[0].shape[0]
    depth, width = panel.shape
    block = depth // blocks
    count = len(strips)
    return pl.pallas_call(
        functools.partial(product_kernel, count),
        out_shape=jax.ShapeDtypeStruct((count, rows, width), jnp.bfloat16),
        grid_spec=pltpu.PrefetchScalarGridSpec(
            num_scalar_prefetch=1,
            grid=(blocks,),
            in_specs=[pl.BlockSpec((rows, block), lambda b, c: (0, c[b]))] * count
            + [pl.BlockSpec((block, width), lambda b, c: (b, 0))],
            out_specs=pl.BlockSpec((count, rows, width), lambda b, c: (0, 0, 0)),
            scratch_shapes=[pltpu.VMEM((count, rows, width), jnp.float32)],
        ),
        compiler_params=pltpu.CompilerParams(dimension_semantics=("arbitrary",)),
        cost_estimate=pl.CostEstimate(
            flops=2 * count * rows * depth * width,
            bytes_accessed=2 * (count * rows * depth + depth * width + count * rows * width),
            transcendentals=0,
        ),
    )(columns, *strips, panel)


def unslice_kernel(pieces, in_ref, out_ref):
    procs = in_ref.shape[1]
    strip = in_ref.shape[3] // pieces
    for a in range(in_ref.shape[0]):
        slices = [in_ref[a, q] for q in range(procs)]
        out_ref[a] = jnp.concatenate(
            [x[:, c * strip : (c + 1) * strip] for c in range(pieces) for x in slices], axis=1
        )


def unslice(moved, pieces):
    count, procs, rows, slice_width = moved.shape
    step = pieces
    return pl.pallas_call(
        functools.partial(unslice_kernel, pieces),
        out_shape=jax.ShapeDtypeStruct((count, rows, procs * slice_width), moved.dtype),
        grid=(count // step,),
        in_specs=[pl.BlockSpec((step, procs, rows, slice_width), lambda i: (i, 0, 0, 0))],
        out_specs=pl.BlockSpec((step, rows, procs * slice_width), lambda i: (i, 0, 0)),
        cost_estimate=pl.CostEstimate(
            flops=0, bytes_accessed=4 * moved.size, transcendentals=0
        ),
    )(moved)


def per_device(
    groups,
    procs,
    ancestor_rows,
    piece_owner,
    structure,
    kept_blocks,
    panel_parent,
    panel_child,
    pivot_parent,
    pivot_child,
):
    f32, bf16 = jnp.float32, jnp.bfloat16
    group_index = lax.axis_index("group")
    proc_index = lax.axis_index("proc")
    owned_count, strip_rows, top_width = ancestor_rows.shape
    blocks = structure.shape[1]
    pieces = panel_parent.shape[2]
    width = panel_parent.shape[-1]
    slice_width = width // procs
    kept = kept_blocks.shape[1]
    own_structure = structure[group_index]
    kept_positions = kept_blocks[group_index]

    order = list(range(0, groups, 2)) + list(range(groups - 1, 0, -2))
    place_of = [order.index(g) for g in range(groups)]
    order_array = jnp.array(order, jnp.int32)
    place_array = jnp.array(place_of, jnp.int32)
    place = place_array[group_index]

    def shift(value, distance):
        pairs = [(order[i], order[(i + distance) % groups]) for i in range(groups)]
        return lax.ppermute(value, "group", pairs)

    def to_slices(panel):
        shape = panel.shape[:-1]
        view = panel.reshape(shape + (pieces, procs, strip_rows))
        return jnp.swapaxes(view, -3, -2).reshape(shape + (procs, slice_width))

    local_parent, local_child = panel_parent[0], panel_child[0]
    positions = jnp.arange(blocks, dtype=jnp.int32)
    match = kept_positions[None, :] == positions[:, None]
    source_block = jnp.sum(match * jnp.arange(1, kept + 1, dtype=jnp.int32)[None, :], axis=1)
    met = jnp.any(match, axis=1)
    placed_child = jnp.where(
        met[:, None, None, None], local_child[source_block], jnp.zeros((), bf16)
    )
    packed = jnp.concatenate([to_slices(local_parent), to_slices(placed_child)], axis=-1)
    panel = lax.all_to_all(packed, "proc", split_axis=3, concat_axis=2, tiled=True)
    panel = panel.reshape(blocks * width, 2 * slice_width)

    panel, ancestor_rows = lax.optimization_barrier((panel, ancestor_rows))
    strips, offsets = [ancestor_rows.reshape(owned_count * strip_rows, top_width)], [0]
    bit = procs // 2
    while bit:
        pairs = [(q, q ^ bit) for q in range(procs)]
        strips = strips + [lax.ppermute(strip, "proc", pairs) for strip in strips]
        offsets = offsets + [offset ^ bit for offset in offsets]
        bit //= 2

    last_strip, panels_after = lax.optimization_barrier(
        (strips[-1], (local_parent, local_child))
    )
    strips = strips[:-1] + [last_strip]
    local_parent, local_child = panels_after
    whole_parent = lax.all_gather(local_parent, "proc", axis=2, tiled=True).reshape(-1, width)
    whole_child = lax.all_gather(local_child, "proc", axis=2, tiled=True).reshape(-1, width)

    def send_home(arrived, distance):
        columns = structure[order_array[(place - distance) % groups]]
        product = structured_product(columns, strips, arrived)
        return shift(product, -distance)

    received = [None] * groups
    received[0] = structured_product(own_structure, strips, panel)
    forth = back = panel
    half = panel.shape[0] // 2
    for distance in range(1, groups // 2):
        forth = shift(forth, 1)
        back = shift(back, -1)
        received[distance] = send_home(forth, distance)
        received[groups - distance] = send_home(back, groups - distance)
    front, rear = forth[:half], back[half:]
    front = shift(front, 1)
    rear = shift(rear, -1)
    opposite = jnp.concatenate([front, rear], axis=0)
    received[groups // 2] = send_home(opposite, groups // 2)

    gathered = jnp.stack(received).reshape(
        groups * procs * owned_count, strip_rows, 2 * slice_width
    )
    wanted = own_structure[:, None] * pieces + jnp.arange(pieces, dtype=jnp.int32)[None, :]
    slab_index = piece_owner[wanted]
    ahead = (place_array[slab_index // owned_count] - place) % groups
    within = slab_index % owned_count
    strip_slot = {offset: j for j, offset in enumerate(offsets)}
    slot_array = jnp.array([strip_slot[offset] for offset in range(procs)], jnp.int32)
    slots = slot_array[jnp.arange(procs, dtype=jnp.int32) ^ proc_index]
    index = (ahead[:, :, None] * procs + slots[None, None, :]) * owned_count + within[:, :, None]
    products = gathered[index.reshape(-1)].reshape(
        blocks, pieces, procs, strip_rows, 2 * slice_width
    )
    column_slice = -products[..., :slice_width]
    inner_slice = products[..., slice_width:]

    def to_strips(value):
        lead = value.shape[:-3]
        moved = lax.all_to_all(
            value, "proc", split_axis=len(lead), concat_axis=len(lead), tiled=True
        )
        flat = moved.reshape((-1,) + moved.shape[-3:])
        return unslice(flat, pieces).reshape(lead + (strip_rows, width))

    both = to_strips(jnp.stack([column_slice, inner_slice]))
    column_parent, inner = both[0], both[1]

    flat_column = column_slice.reshape(blocks * width, slice_width)
    product_block = lax.dot_general(
        whole_parent, flat_column, (((0,), (0,)), ((), ())), preferred_element_type=f32
    )
    pivot_slice = pivot_parent[0].reshape(slice_width, width).T
    block_slice = (pivot_slice.astype(f32) - product_block).astype(bf16)
    block_parent = to_strips(block_slice.reshape(pieces, procs, strip_rows, slice_width))

    head_slice = jnp.concatenate(
        [
            block_slice[None],
            column_slice.reshape(blocks, width, slice_width)[kept_positions],
        ],
        axis=0,
    ).reshape(-1, slice_width)
    first_rows = lax.dot_general(
        head_slice, whole_child, (((0,), (0,)), ((), ())), preferred_element_type=f32
    ).reshape(1, pieces, strip_rows, width)

    head_rows = column_parent[kept_positions].reshape(-1, width)
    outer = jnp.dot(head_rows, whole_child[:width], preferred_element_type=f32)
    rest = outer.reshape(kept, pieces, strip_rows, width) + inner[kept_positions].astype(f32)
    column_child = (-jnp.concatenate([first_rows, rest], axis=0)).astype(bf16)

    partial = lax.dot_general(
        local_child.reshape(-1, width),
        column_child.reshape(-1, width),
        (((0,), (0,)), ((), ())),
        preferred_element_type=f32,
    ).astype(bf16)
    partial = lax.all_to_all(
        partial.reshape(pieces, procs, strip_rows, width),
        "proc",
        split_axis=1,
        concat_axis=1,
        tiled=True,
    )
    summed = jnp.sum(partial.astype(f32), axis=1)
    block_child = (pivot_child[0].astype(f32) - summed).astype(bf16)
    return column_parent[None], block_parent[None], column_child[None], block_child[None]


def solution(mesh):
    in_specs = (
        P("group", "proc", None),
        P(),
        P(),
        P(),
        P("group", None, None, "proc", None),
        P("group", None, None, "proc", None),
        P("group", None, "proc", None),
        P("group", None, "proc", None),
    )
    out_specs = (
        P("group", None, None, "proc", None),
        P("group", None, "proc", None),
        P("group", None, None, "proc", None),
        P("group", None, "proc", None),
    )
    groups = mesh.shape["group"]

    def body(*args):
        return per_device(groups, mesh.shape["proc"], *args)

    return jax.shard_map(
        body, mesh=mesh, in_specs=in_specs, out_specs=out_specs, check_vma=False
    )
```

```python
import functools
import math

import jax
import jax.numpy as jnp
from jax import lax
from jax.experimental import pallas as pl
from jax.experimental.pallas import tpu as pltpu
from jax.sharding import PartitionSpec as P


def product_kernel(strip_count, columns_ref, *refs):
    strips, panel_ref = refs[:strip_count], refs[strip_count]
    out_ref, total = refs[strip_count + 1 :]
    step = pl.program_id(0)

    @pl.when(step == 0)
    def _():
        total[...] = jnp.zeros_like(total)

    panel = panel_ref[...]
    for j, strip in enumerate(strips):
        total[j] += jnp.dot(strip[...], panel, preferred_element_type=jnp.float32)

    @pl.when(step == pl.num_programs(0) - 1)
    def _():
        out_ref[...] = total[...].astype(out_ref.dtype)


def structured_product(columns, strips, panel):
    blocks = columns.shape[0]
    rows = strips[0].shape[0]
    depth, width = panel.shape
    block = depth // blocks
    count = len(strips)
    return pl.pallas_call(
        functools.partial(product_kernel, count),
        out_shape=jax.ShapeDtypeStruct((count, rows, width), jnp.bfloat16),
        grid_spec=pltpu.PrefetchScalarGridSpec(
            num_scalar_prefetch=1,
            grid=(blocks,),
            in_specs=[pl.BlockSpec((rows, block), lambda b, c: (0, c[b]))] * count
            + [pl.BlockSpec((block, width), lambda b, c: (b, 0))],
            out_specs=pl.BlockSpec((count, rows, width), lambda b, c: (0, 0, 0)),
            scratch_shapes=[pltpu.VMEM((count, rows, width), jnp.float32)],
        ),
        compiler_params=pltpu.CompilerParams(dimension_semantics=("arbitrary",)),
        cost_estimate=pl.CostEstimate(
            flops=2 * count * rows * depth * width,
            bytes_accessed=2 * (count * rows * depth + depth * width + count * rows * width),
            transcendentals=0,
        ),
    )(columns, *strips, panel)


def pack_kernel(source_ref, met_ref, parent_ref, child_ref, out_ref):
    pieces, _, width = parent_ref.shape[1:]
    procs = out_ref.shape[0]
    part = width // (pieces * procs)
    met = met_ref[pl.program_id(0)] > 0
    for a in range(pieces):
        parent = parent_ref[0, a]
        child = child_ref[0, a]
        child = jnp.where(met, child, jnp.zeros_like(child))
        for q in range(procs):
            out_ref[q, 0, a] = jnp.concatenate(
                [
                    panel[:, (c * procs + q) * part : (c * procs + q + 1) * part]
                    for panel in (parent, child)
                    for c in range(pieces)
                ],
                axis=1,
            )


def pack(source_block, met, parent, child, procs):
    blocks, pieces, strip, width = parent.shape
    return pl.pallas_call(
        pack_kernel,
        out_shape=jax.ShapeDtypeStruct(
            (procs, blocks, pieces, strip, 2 * width // procs), parent.dtype
        ),
        grid_spec=pltpu.PrefetchScalarGridSpec(
            num_scalar_prefetch=2,
            grid=(blocks,),
            in_specs=[
                pl.BlockSpec((1, pieces, strip, width), lambda b, s, m: (b, 0, 0, 0)),
                pl.BlockSpec((1, pieces, strip, width), lambda b, s, m: (s[b], 0, 0, 0)),
            ],
            out_specs=pl.BlockSpec(
                (procs, 1, pieces, strip, 2 * width // procs), lambda b, s, m: (0, b, 0, 0, 0)
            ),
        ),
    )(source_block, met, parent, child)


def unslice_kernel(pieces, in_ref, out_ref):
    procs = in_ref.shape[1]
    strip = in_ref.shape[3] // pieces
    for a in range(in_ref.shape[0]):
        slices = [in_ref[a, q] for q in range(procs)]
        out_ref[a] = jnp.concatenate(
            [x[:, c * strip : (c + 1) * strip] for c in range(pieces) for x in slices], axis=1
        )


def unslice(moved, pieces):
    count, procs, rows, slice_width = moved.shape
    step = math.gcd(count, 8)
    return pl.pallas_call(
        functools.partial(unslice_kernel, pieces),
        out_shape=jax.ShapeDtypeStruct((count, rows, procs * slice_width), moved.dtype),
        grid=(count // step,),
        in_specs=[pl.BlockSpec((step, procs, rows, slice_width), lambda i: (i, 0, 0, 0))],
        out_specs=pl.BlockSpec((step, rows, procs * slice_width), lambda i: (i, 0, 0)),
        cost_estimate=pl.CostEstimate(
            flops=0, bytes_accessed=4 * moved.size, transcendentals=0
        ),
    )(moved)


def per_device(
    groups,
    procs,
    ancestor_rows,
    piece_owner,
    structure,
    kept_blocks,
    panel_parent,
    panel_child,
    pivot_parent,
    pivot_child,
):
    f32, bf16 = jnp.float32, jnp.bfloat16
    group_index = lax.axis_index("group")
    proc_index = lax.axis_index("proc")
    owned_count, strip_rows, top_width = ancestor_rows.shape
    blocks = structure.shape[1]
    pieces = panel_parent.shape[2]
    width = panel_parent.shape[-1]
    slice_width = width // procs
    kept = kept_blocks.shape[1]
    own_structure = structure[group_index]
    kept_positions = kept_blocks[group_index]

    order = list(range(0, groups, 2)) + list(range(groups - 1, 0, -2))
    place_of = [order.index(g) for g in range(groups)]
    order_array = jnp.array(order, jnp.int32)
    place_array = jnp.array(place_of, jnp.int32)
    place = place_array[group_index]

    def shift(value, distance):
        pairs = [(order[i], order[(i + distance) % groups]) for i in range(groups)]
        return lax.ppermute(value, "group", pairs)

    local_parent, local_child = panel_parent[0], panel_child[0]
    positions = jnp.arange(blocks, dtype=jnp.int32)
    match = kept_positions[None, :] == positions[:, None]
    source_block = jnp.sum(match * jnp.arange(1, kept + 1, dtype=jnp.int32)[None, :], axis=1)
    met = jnp.any(match, axis=1)
    packed = pack(
        source_block.astype(jnp.int32), met.astype(jnp.int32), local_parent, local_child, procs
    )
    panel = lax.all_to_all(packed, "proc", split_axis=0, concat_axis=0, tiled=True)
    panel = jnp.moveaxis(panel, 0, 2)
    panel = panel.reshape(blocks * width, 2 * slice_width)

    panel, ancestor_rows = lax.optimization_barrier((panel, ancestor_rows))
    strips, offsets = [ancestor_rows.reshape(owned_count * strip_rows, top_width)], [0]
    bit = procs // 2
    while bit:
        pairs = [(q, q ^ bit) for q in range(procs)]
        arrived = []
        for strip in strips:
            arrived.append(lax.ppermute(strip, "proc", pairs))
        strips = strips + arrived
        offsets = offsets + [offset ^ bit for offset in offsets]
        bit //= 2

    def send_home(arrived, distance):
        columns = structure[order_array[(place - distance) % groups]]
        product = structured_product(columns, strips, arrived)
        return shift(product, -distance)

    received = [None] * groups
    received[0] = structured_product(own_structure, strips, panel)
    received[0], panels_after = lax.optimization_barrier(
        (received[0], (local_parent, local_child))
    )
    local_parent, local_child = panels_after
    whole_parent = lax.all_gather(local_parent, "proc", axis=2, tiled=True).reshape(-1, width)
    whole_child = lax.all_gather(local_child, "proc", axis=2, tiled=True).reshape(-1, width)
    forth = back = panel
    half = panel.shape[0] // 2
    for distance in range(1, groups // 2):
        forth = shift(forth, 1)
        back = shift(back, -1)
        received[distance] = send_home(forth, distance)
        received[groups - distance] = send_home(back, groups - distance)
    front, rear = forth[:half], back[half:]
    front = shift(front, 1)
    rear = shift(rear, -1)
    opposite = jnp.concatenate([front, rear], axis=0)
    received[groups // 2] = send_home(opposite, groups // 2)

    gathered = jnp.stack(received).reshape(
        groups * procs * owned_count, strip_rows, 2 * slice_width
    )
    wanted = own_structure[:, None] * pieces + jnp.arange(pieces, dtype=jnp.int32)[None, :]
    slab_index = piece_owner[wanted]
    ahead = (place_array[slab_index // owned_count] - place) % groups
    within = slab_index % owned_count
    strip_slot = {offset: j for j, offset in enumerate(offsets)}
    slot_array = jnp.array([strip_slot[offset] for offset in range(procs)], jnp.int32)
    slots = slot_array[jnp.arange(procs, dtype=jnp.int32) ^ proc_index]
    index = (ahead[:, :, None] * procs + slots[None, None, :]) * owned_count + within[:, :, None]
    products = gathered[index.reshape(-1)].reshape(
        blocks, pieces, procs, strip_rows, 2 * slice_width
    )
    column_slice = -products[..., :slice_width]
    inner_slice = products[..., slice_width:]

    def to_strips(value):
        lead = value.shape[:-3]
        moved = lax.all_to_all(
            value, "proc", split_axis=len(lead), concat_axis=len(lead), tiled=True
        )
        flat = moved.reshape((-1,) + moved.shape[-3:])
        return unslice(flat, pieces).reshape(lead + (strip_rows, width))

    both = to_strips(jnp.stack([column_slice, inner_slice]))
    column_parent, inner = both[0], both[1]

    flat_column = column_slice.reshape(blocks * width, slice_width)
    product_block = lax.dot_general(
        whole_parent, flat_column, (((0,), (0,)), ((), ())), preferred_element_type=f32
    )
    pivot_slice = pivot_parent[0].reshape(slice_width, width).T
    block_slice = (pivot_slice.astype(f32) - product_block).astype(bf16)
    block_parent = to_strips(block_slice.reshape(pieces, procs, strip_rows, slice_width))

    head_slice = jnp.concatenate(
        [
            block_slice[None],
            column_slice.reshape(blocks, width, slice_width)[kept_positions],
        ],
        axis=0,
    ).reshape(-1, slice_width)
    first_rows = lax.dot_general(
        head_slice, whole_child, (((0,), (0,)), ((), ())), preferred_element_type=f32
    ).reshape(1, pieces, strip_rows, width)

    head_rows = column_parent[kept_positions].reshape(-1, width)
    outer = jnp.dot(head_rows, whole_child[:width], preferred_element_type=f32)
    rest = outer.reshape(kept, pieces, strip_rows, width) + inner[kept_positions].astype(f32)
    column_child = (-jnp.concatenate([first_rows, rest], axis=0)).astype(bf16)

    partial = lax.dot_general(
        local_child.reshape(-1, width),
        column_child.reshape(-1, width),
        (((0,), (0,)), ((), ())),
        preferred_element_type=f32,
    ).astype(bf16)
    partial = lax.all_to_all(
        partial.reshape(pieces, procs, strip_rows, width),
        "proc",
        split_axis=1,
        concat_axis=1,
        tiled=True,
    )
    summed = jnp.sum(partial.astype(f32), axis=1)
    block_child = (pivot_child[0].astype(f32) - summed).astype(bf16)
    return column_parent[None], block_parent[None], column_child[None], block_child[None]


def solution(mesh):
    in_specs = (
        P("group", "proc", None),
        P(),
        P(),
        P(),
        P("group", None, None, "proc", None),
        P("group", None, None, "proc", None),
        P("group", None, "proc", None),
        P("group", None, "proc", None),
    )
    out_specs = (
        P("group", None, None, "proc", None),
        P("group", None, "proc", None),
        P("group", None, None, "proc", None),
        P("group", None, "proc", None),
    )
    groups = mesh.shape["group"]

    def body(*args):
        return per_device(groups, mesh.shape["proc"], *args)

    return jax.shard_map(
        body, mesh=mesh, in_specs=in_specs, out_specs=out_specs, check_vma=False
    )
```

```python
import functools
import math

import jax
import jax.numpy as jnp
from jax import lax
from jax.experimental import pallas as pl
from jax.experimental.pallas import tpu as pltpu
from jax.sharding import PartitionSpec as P


def product_kernel(strip_count, columns_ref, *refs):
    strips, panel_ref = refs[:strip_count], refs[strip_count]
    out_ref, total = refs[strip_count + 1 :]
    step = pl.program_id(0)

    @pl.when(step == 0)
    def _():
        total[...] = jnp.zeros_like(total)

    panel = panel_ref[...]
    for j, strip in enumerate(strips):
        total[j] += jnp.dot(strip[...], panel, preferred_element_type=jnp.float32)

    @pl.when(step == pl.num_programs(0) - 1)
    def _():
        out_ref[...] = total[...].astype(out_ref.dtype)


def structured_product(columns, strips, panel):
    blocks = columns.shape[0]
    rows = strips[0].shape[0]
    depth, width = panel.shape
    block = depth // blocks
    count = len(strips)
    return pl.pallas_call(
        functools.partial(product_kernel, count),
        out_shape=jax.ShapeDtypeStruct((count, rows, width), jnp.bfloat16),
        grid_spec=pltpu.PrefetchScalarGridSpec(
            num_scalar_prefetch=1,
            grid=(blocks,),
            in_specs=[pl.BlockSpec((rows, block), lambda b, c: (0, c[b]))] * count
            + [pl.BlockSpec((block, width), lambda b, c: (b, 0))],
            out_specs=pl.BlockSpec((count, rows, width), lambda b, c: (0, 0, 0)),
            scratch_shapes=[pltpu.VMEM((count, rows, width), jnp.float32)],
        ),
        compiler_params=pltpu.CompilerParams(dimension_semantics=("arbitrary",)),
        cost_estimate=pl.CostEstimate(
            flops=2 * count * rows * depth * width,
            bytes_accessed=2 * (count * rows * depth + depth * width + count * rows * width),
            transcendentals=0,
        ),
    )(columns, *strips, panel)


def pack_kernel(source_ref, met_ref, parent_ref, child_ref, out_ref):
    pieces, _, width = parent_ref.shape[1:]
    procs = out_ref.shape[0]
    part = width // (pieces * procs)
    met = met_ref[pl.program_id(0)] > 0
    for a in range(pieces):
        parent = parent_ref[0, a]
        child = child_ref[0, a]
        child = jnp.where(met, child, jnp.zeros_like(child))
        for q in range(procs):
            out_ref[q, 0, a] = jnp.concatenate(
                [
                    panel[:, (c * procs + q) * part : (c * procs + q + 1) * part]
                    for panel in (parent, child)
                    for c in range(pieces)
                ],
                axis=1,
            )


def pack(source_block, met, parent, child, procs):
    blocks, pieces, strip, width = parent.shape
    return pl.pallas_call(
        pack_kernel,
        out_shape=jax.ShapeDtypeStruct(
            (procs, blocks, pieces, strip, 2 * width // procs), parent.dtype
        ),
        grid_spec=pltpu.PrefetchScalarGridSpec(
            num_scalar_prefetch=2,
            grid=(blocks,),
            in_specs=[
                pl.BlockSpec((1, pieces, strip, width), lambda b, s, m: (b, 0, 0, 0)),
                pl.BlockSpec((1, pieces, strip, width), lambda b, s, m: (s[b], 0, 0, 0)),
            ],
            out_specs=pl.BlockSpec(
                (procs, 1, pieces, strip, 2 * width // procs), lambda b, s, m: (0, b, 0, 0, 0)
            ),
        ),
    )(source_block, met, parent, child)


def unslice_kernel(pieces, in_ref, out_ref):
    procs = in_ref.shape[1]
    strip = in_ref.shape[3] // pieces
    for a in range(in_ref.shape[0]):
        slices = [in_ref[a, q] for q in range(procs)]
        out_ref[a] = jnp.concatenate(
            [x[:, c * strip : (c + 1) * strip] for c in range(pieces) for x in slices], axis=1
        )


def unslice(moved, pieces):
    count, procs, rows, slice_width = moved.shape
    step = math.gcd(count, 8)
    return pl.pallas_call(
        functools.partial(unslice_kernel, pieces),
        out_shape=jax.ShapeDtypeStruct((count, rows, procs * slice_width), moved.dtype),
        grid=(count // step,),
        in_specs=[pl.BlockSpec((step, procs, rows, slice_width), lambda i: (i, 0, 0, 0))],
        out_specs=pl.BlockSpec((step, rows, procs * slice_width), lambda i: (i, 0, 0)),
        cost_estimate=pl.CostEstimate(
            flops=0, bytes_accessed=4 * moved.size, transcendentals=0
        ),
    )(moved)


def per_device(
    groups,
    procs,
    ancestor_rows,
    piece_owner,
    structure,
    kept_blocks,
    panel_parent,
    panel_child,
    pivot_parent,
    pivot_child,
):
    f32, bf16 = jnp.float32, jnp.bfloat16
    group_index = lax.axis_index("group")
    proc_index = lax.axis_index("proc")
    owned_count, strip_rows, top_width = ancestor_rows.shape
    blocks = structure.shape[1]
    pieces = panel_parent.shape[2]
    width = panel_parent.shape[-1]
    slice_width = width // procs
    kept = kept_blocks.shape[1]
    own_structure = structure[group_index]
    kept_positions = kept_blocks[group_index]

    order = list(range(0, groups, 2)) + list(range(groups - 1, 0, -2))
    place_of = [order.index(g) for g in range(groups)]
    order_array = jnp.array(order, jnp.int32)
    place_array = jnp.array(place_of, jnp.int32)
    place = place_array[group_index]

    def shift(value, distance):
        pairs = [(order[i], order[(i + distance) % groups]) for i in range(groups)]
        return lax.ppermute(value, "group", pairs)

    local_parent, local_child = panel_parent[0], panel_child[0]
    positions = jnp.arange(blocks, dtype=jnp.int32)
    match = kept_positions[None, :] == positions[:, None]
    source_block = jnp.sum(match * jnp.arange(1, kept + 1, dtype=jnp.int32)[None, :], axis=1)
    met = jnp.any(match, axis=1)
    packed = pack(
        source_block.astype(jnp.int32), met.astype(jnp.int32), local_parent, local_child, procs
    )
    panel = lax.all_to_all(packed, "proc", split_axis=0, concat_axis=0, tiled=True)
    panel = jnp.moveaxis(panel, 0, 2)
    panel = panel.reshape(blocks * width, 2 * slice_width)

    panel, ancestor_rows = lax.optimization_barrier((panel, ancestor_rows))
    strips, offsets = [ancestor_rows.reshape(owned_count * strip_rows, top_width)], [0]
    bit = procs // 2
    while bit:
        pairs = [(q, q ^ bit) for q in range(procs)]
        arrived = []
        for strip in strips:
            arrived.append(lax.ppermute(strip, "proc", pairs))
        strips = strips + arrived
        offsets = offsets + [offset ^ bit for offset in offsets]
        bit //= 2

    strip_slot = {offset: j for j, offset in enumerate(offsets)}
    slot_array = jnp.array([strip_slot[offset] for offset in range(procs)], jnp.int32)
    slots = slot_array[jnp.arange(procs, dtype=jnp.int32) ^ proc_index]

    def gather_rows(panel_rows):
        parts, bit = [panel_rows], procs // 2
        while bit:
            pairs = [(q, q ^ bit) for q in range(procs)]
            parts = parts + [lax.ppermute(part, "proc", pairs) for part in parts]
            bit //= 2
        return jnp.moveaxis(jnp.stack(parts)[slots], 0, 2).reshape(-1, width)

    def send_home(arrived, distance):
        columns = structure[order_array[(place - distance) % groups]]
        product = structured_product(columns, strips, arrived)
        return shift(product, -distance)

    received = [None] * groups
    received[0] = structured_product(own_structure, strips, panel)
    received[0], panels_after = lax.optimization_barrier(
        (received[0], (local_parent, local_child))
    )
    local_parent, local_child = panels_after
    whole_parent, whole_child = gather_rows(local_parent), gather_rows(local_child)
    forth = back = panel
    half = panel.shape[0] // 2
    for distance in range(1, groups // 2):
        forth = shift(forth, 1)
        back = shift(back, -1)
        received[distance] = send_home(forth, distance)
        received[groups - distance] = send_home(back, groups - distance)
    front, rear = forth[:half], back[half:]
    front = shift(front, 1)
    rear = shift(rear, -1)
    opposite = jnp.concatenate([front, rear], axis=0)
    received[groups // 2] = send_home(opposite, groups // 2)

    gathered = jnp.stack(received).reshape(
        groups * procs * owned_count, strip_rows, 2 * slice_width
    )
    wanted = own_structure[:, None] * pieces + jnp.arange(pieces, dtype=jnp.int32)[None, :]
    slab_index = piece_owner[wanted]
    ahead = (place_array[slab_index // owned_count] - place) % groups
    within = slab_index % owned_count
    index = (ahead[:, :, None] * procs + slots[None, None, :]) * owned_count + within[:, :, None]
    products = gathered[index.reshape(-1)].reshape(
        blocks, pieces, procs, strip_rows, 2 * slice_width
    )
    column_slice = -products[..., :slice_width]
    inner_slice = products[..., slice_width:]

    def to_strips(value):
        lead = value.shape[:-3]
        moved = lax.all_to_all(
            value, "proc", split_axis=len(lead), concat_axis=len(lead), tiled=True
        )
        flat = moved.reshape((-1,) + moved.shape[-3:])
        return unslice(flat, pieces).reshape(lead + (strip_rows, width))

    both = to_strips(jnp.stack([column_slice, inner_slice]))
    column_parent, inner = both[0], both[1]

    flat_column = column_slice.reshape(blocks * width, slice_width)
    product_block = lax.dot_general(
        whole_parent, flat_column, (((0,), (0,)), ((), ())), preferred_element_type=f32
    )
    pivot_slice = pivot_parent[0].reshape(slice_width, width).T
    block_slice = (pivot_slice.astype(f32) - product_block).astype(bf16)
    block_parent = to_strips(block_slice.reshape(pieces, procs, strip_rows, slice_width))

    head_slice = jnp.concatenate(
        [
            block_slice[None],
            column_slice.reshape(blocks, width, slice_width)[kept_positions],
        ],
        axis=0,
    ).reshape(-1, slice_width)
    first_rows = lax.dot_general(
        head_slice, whole_child, (((0,), (0,)), ((), ())), preferred_element_type=f32
    ).reshape(1, pieces, strip_rows, width)

    head_rows = column_parent[kept_positions].reshape(-1, width)
    outer = jnp.dot(head_rows, whole_child[:width], preferred_element_type=f32)
    rest = outer.reshape(kept, pieces, strip_rows, width) + inner[kept_positions].astype(f32)
    column_child = (-jnp.concatenate([first_rows, rest], axis=0)).astype(bf16)

    partial = lax.dot_general(
        local_child.reshape(-1, width),
        column_child.reshape(-1, width),
        (((0,), (0,)), ((), ())),
        preferred_element_type=f32,
    ).astype(bf16)
    partial = lax.all_to_all(
        partial.reshape(pieces, procs, strip_rows, width),
        "proc",
        split_axis=1,
        concat_axis=1,
        tiled=True,
    )
    summed = jnp.sum(partial.astype(f32), axis=1)
    block_child = (pivot_child[0].astype(f32) - summed).astype(bf16)
    return column_parent[None], block_parent[None], column_child[None], block_child[None]


def solution(mesh):
    in_specs = (
        P("group", "proc", None),
        P(),
        P(),
        P(),
        P("group", None, None, "proc", None),
        P("group", None, None, "proc", None),
        P("group", None, "proc", None),
        P("group", None, "proc", None),
    )
    out_specs = (
        P("group", None, None, "proc", None),
        P("group", None, "proc", None),
        P("group", None, None, "proc", None),
        P("group", None, "proc", None),
    )
    groups = mesh.shape["group"]

    def body(*args):
        return per_device(groups, mesh.shape["proc"], *args)

    return jax.shard_map(
        body, mesh=mesh, in_specs=in_specs, out_specs=out_specs, check_vma=False
    )
```
